32 devices in a mesh: frame: 8 (over z, core), head: 4 (over y, x).
Axes of the slice: x: 2, y: 2, z: 4, core: 2. Of those that a mesh axis runs over, the one named last changes fastest.
Arguments:
- queries: bfloat16 [4096, 1024], P('frame', 'head'), may hold values from -6 to 6
- key_rows: bfloat16 [4096, 1024], P('frame', 'head'), may hold values from -6 to 6
- values: bfloat16 [4096, 1024], P('frame', 'head'), may hold values from -6 to 6
- gate_init: float32 [8, 128, 128], P('head'), may hold values from -0.5 to 0.5
- up_init: float32 [8, 128, 128], P('head'), may hold values from -0.5 to 0.5
- down_init: float32 [8, 128, 128], P('head'), may hold values from -0.5 to 0.5
- step_size: float32 [8], P('head'), may hold values from 0.1 to 1
- head_scale: float32 [8], P('head'), may hold values from 0.25 to 4
- out_gain: float32 [1024], P('head'), may hold values from 0.5 to 1.5
Outputs:
- layer_out: bfloat16 [4096, 1024], P('frame', 'head')
The draws below stay inside these ranges and needn't reach their ends.
All inputs are finite; a program needn't handle non-finite values.
Results may differ from the reference program's by a relative error of at most 0.012.
The reference program's roundings to bfloat16 on the way (of `probs`, `attended`, `query_norm` and `fast_out`) count: a program that leaves them out, or rounds other values in their place, can miss the bound.
Values may be sent and summed in bfloat16 or wider, within the bound.
A program may use at most 64 MiB of HBM per device.

```python
import math
import jax
import jax.numpy as jnp
from jax import lax

DH = 128
FWH = 128
FT = 512
NS_ITERS = 5
GROUPS = 2
HEADS = 8
TOKENS = 4096
N_FRAME = 8


def drawn_pair(key):
    base = jax.random.fold_in(key, 4111)
    width = HEADS * DH
    shape = (TOKENS, width)
    query_draw = jnp.clip(jax.random.normal(jax.random.fold_in(base, 1), shape, jnp.float32), -4.0, 4.0)
    key_draw = jnp.clip(jax.random.normal(jax.random.fold_in(base, 2), shape, jnp.float32), -4.0, 4.0)
    return (query_draw, key_draw)


def draw_queries(key, part):
    return drawn_pair(key)[0].astype(jnp.bfloat16)


def draw_key_rows(key, part):
    return drawn_pair(key)[1].astype(jnp.bfloat16)


def block_levels(key, dims, pieces, low, high):
    loudness = 1.0
    for axis_at, shards_of in pieces:
        steps = jax.random.uniform(jax.random.fold_in(jax.random.fold_in(key, 6), axis_at), (shards_of,), jnp.float32, low / len(pieces), high / len(pieces))
        loudness = loudness * jnp.repeat(jnp.exp(steps), dims[axis_at] // shards_of).reshape((-1,) + (1,) * (len(dims) - 1 - axis_at))
    return loudness


def centred(rng, dims, scale, limit, split=(), kind=jnp.bfloat16):
    values = scale * jax.random.normal(rng, dims, jnp.float32)
    if split:
        values = values * block_levels(rng, dims, split, -0.22, 0.18)
    return jnp.clip(values, -limit, limit).astype(kind)


def setup_inputs(seed: int = 0) -> dict:
    splits = jax.random.split(jax.random.key(seed), 10)
    queries = draw_queries(jax.random.fold_in(splits[9], 71), 0)
    key_rows = draw_key_rows(jax.random.fold_in(splits[9], 71), 0)
    values = centred(splits[2], (TOKENS, HEADS * DH), 1.0, 6.0, ((0, 8), (1, 4)))
    gate_init = centred(splits[3], (HEADS, DH, FWH), DH ** -0.5, 0.5, ((0, 4),), jnp.float32)
    up_init = centred(splits[4], (HEADS, DH, FWH), DH ** -0.5, 0.5, ((0, 4),), jnp.float32)
    down_init = centred(splits[5], (HEADS, FWH, DH), FWH ** -0.5, 0.5, ((0, 4),), jnp.float32)
    step_size = jnp.clip(jnp.exp(math.log(1.0) - 2.3025851 * jax.random.uniform(splits[6], (HEADS,), jnp.float32) ** block_levels(splits[6], (HEADS,), ((0, 4),), -0.2, 0.2)), 0.1, 1.0)
    head_scale = jnp.clip(jnp.exp(math.log(4.0) - 2.7725887 * jax.random.uniform(splits[7], (HEADS,), jnp.float32) ** block_levels(splits[7], (HEADS,), ((0, 4),), -0.2, 0.2)), 0.25, 4.0)
    out_gain = jnp.clip(1.0 + 0.1 * jax.random.normal(splits[8], (HEADS * DH,), jnp.float32), 0.5, 1.5)
    return {"queries": queries, "key_rows": key_rows, "values": values, "gate_init": gate_init, "up_init": up_init, "down_init": down_init, "step_size": step_size, "head_scale": head_scale, "out_gain": out_gain}


quintic_terms = (3.4445, -4.775, 2.0315)
highest = lax.Precision.HIGHEST

def rms_scale(rows_in, epsilon):
    mean_square = lax.optimization_barrier(jnp.mean(rows_in * rows_in, axis=-1, keepdims=True))
    return rows_in * lax.rsqrt(mean_square + epsilon)

def newton_schulz(gradient):
    flipped = gradient.shape[1] > gradient.shape[2]
    matrix = jnp.swapaxes(gradient, 1, 2) if flipped else gradient
    frobenius = jnp.sqrt(lax.optimization_barrier(jnp.sum(matrix * matrix, axis=(1, 2), keepdims=True)))
    matrix = matrix / (frobenius + 1e-07)
    for repeat_no in range(NS_ITERS):
        square = jnp.einsum('hij,hkj->hik', matrix, matrix, precision=highest)
        quartic = jnp.einsum('hij,hjk->hik', square, square, precision=highest)
        mixing = quintic_terms[1] * square + quintic_terms[2] * quartic
        matrix = quintic_terms[0] * matrix + jnp.einsum('hij,hjk->hik', mixing, matrix, precision=highest)
    return jnp.swapaxes(matrix, 1, 2) if flipped else matrix

def column_norms(weight):
    return jnp.sqrt(lax.optimization_barrier(jnp.sum(weight * weight, axis=1, keepdims=True)))

def fast_grads(weights, key_part, value_part):
    gate_w, up_w, down_w = weights
    key_f = key_part.astype(jnp.float32)
    value_f = value_part.astype(jnp.float32)
    gate = jnp.einsum('nhd,hdf->nhf', key_f, gate_w, precision=highest)
    upward = jnp.einsum('nhd,hdf->nhf', key_f, up_w, precision=highest)
    sigma = jax.nn.sigmoid(gate)
    active = gate * sigma
    hidden = active * upward
    back_hidden = -jnp.einsum('nhd,hfd->nhf', value_f, down_w, precision=highest)
    grad_down = -jnp.einsum('nhf,nhd->hfd', hidden, value_f, precision=highest)
    back_gate = back_hidden * upward * sigma * (1.0 + gate * (1.0 - sigma))
    back_up = back_hidden * active
    grad_gate = jnp.einsum('nhd,nhf->hdf', key_f, back_gate, precision=highest)
    grad_up = jnp.einsum('nhd,nhf->hdf', key_f, back_up, precision=highest)
    return (grad_gate, grad_up, grad_down)

def renewed(weights, gradients, step_size, targets):
    result = []
    for weight, gradient, target in zip(weights, gradients, targets):
        moved = weight - step_size[:, None, None] * newton_schulz(gradient)
        length = jnp.sqrt(lax.optimization_barrier(jnp.sum(moved * moved, axis=1, keepdims=True)))
        result.append(moved * (target / (length + 1e-06)))
    return tuple(result)

def fast_apply(weights, query_part, head_scale):
    gate_w, up_w, down_w = weights
    query_f = query_part.astype(jnp.float32)
    gate = jnp.einsum('nhd,hdf->nhf', query_f, gate_w, precision=highest)
    upward = jnp.einsum('nhd,hdf->nhf', query_f, up_w, precision=highest)
    hidden = jax.nn.silu(gate) * upward
    output = jnp.einsum('nhf,hfd->nhd', hidden, down_w, precision=highest)
    return (output * head_scale[None, :, None]).astype(jnp.bfloat16)

def reference(queries, key_rows, values, gate_init, up_init, down_init, step_size, head_scale, out_gain):
    frames = N_FRAME
    heads = HEADS
    grid_q = queries.reshape(frames, FT, heads, DH).transpose(0, 2, 1, 3)
    grid_k = key_rows.reshape(frames, FT, heads, DH).transpose(0, 2, 1, 3)
    grid_v = values.reshape(frames, FT, heads, DH).transpose(0, 2, 1, 3)
    score_scale = 1.0 / math.sqrt(DH)
    column = lax.broadcasted_iota(jnp.int32, (1, 2 * FT), 1)

    def one_pair(index):
        frame_no = index // heads
        head_no = index % heads
        prev_no = jnp.maximum(frame_no - 1, 0)
        query_part = grid_q[frame_no, head_no].astype(jnp.float32)
        key_all = jnp.concatenate([grid_k[prev_no, head_no], grid_k[frame_no, head_no]], axis=0).astype(jnp.float32)
        value_all = jnp.concatenate([grid_v[prev_no, head_no], grid_v[frame_no, head_no]], axis=0).astype(jnp.float32)
        scores = jnp.einsum('qd,kd->qk', query_part, key_all) * score_scale
        masked = jnp.logical_and(frame_no == 0, column < FT)
        scores = jnp.where(masked, -1e+30, scores)
        probs = jax.nn.softmax(scores, axis=-1).astype(jnp.bfloat16)
        probs = lax.optimization_barrier(probs).astype(jnp.float32)
        mixed = jnp.einsum('qk,kd->qd', probs, value_all)
        return rms_scale(mixed, 1e-06).astype(jnp.bfloat16)
    attended = lax.map(one_pair, jnp.arange(frames * heads, dtype=jnp.int32))
    attended = attended.reshape(frames, heads, FT, DH).transpose(0, 2, 1, 3).reshape(TOKENS, heads, DH)
    query_norm = rms_scale(queries.astype(jnp.float32).reshape(TOKENS, heads, DH), 1e-06).astype(jnp.bfloat16)
    value_grid = values.reshape(TOKENS, heads, DH)
    seg_len = TOKENS // GROUPS

    def per_head(packed):
        key_h, query_h, value_h, gate_w, up_w, down_w, step_h, scale_h = packed
        weights = (gate_w[None], up_w[None], down_w[None])
        targets = tuple((column_norms(weight) for weight in weights))
        outputs = []
        for segment in range(GROUPS):
            lower = segment * seg_len
            upper = lower + seg_len
            gradients = fast_grads(weights, key_h[lower:upper][:, None], value_h[lower:upper][:, None])
            weights = renewed(weights, gradients, step_h[None], targets)
            outputs.append(fast_apply(weights, query_h[lower:upper][:, None], scale_h[None])[:, 0])
        return jnp.concatenate(outputs, axis=0)
    fast_out = lax.map(per_head, (attended.transpose(1, 0, 2), query_norm.transpose(1, 0, 2), value_grid.transpose(1, 0, 2), gate_init, up_init, down_init, step_size, head_scale))
    fast_out = fast_out.transpose(1, 0, 2).reshape(TOKENS, heads * DH)
    combined = attended.reshape(TOKENS, heads * DH).astype(jnp.float32) + fast_out.astype(jnp.float32)
    total = lax.optimization_barrier(jnp.mean(combined * combined, axis=1, keepdims=True))
    return (combined * lax.rsqrt(total + 1e-05) * out_gain[None, :]).astype(jnp.bfloat16)
```

```python
import functools
import math

import jax
import jax.numpy as jnp
from jax import lax
from jax.experimental import pallas as pl
from jax.experimental.pallas import tpu as pltpu
from jax.sharding import PartitionSpec as P

NS_ITERS = 5
GROUPS = 2
MESH = pl.DeviceIdType.MESH
SENT = jnp.bfloat16
COARSE = 2
BF = jnp.bfloat16
F32 = jnp.float32
quintic_terms = (3.4445, -4.775, 2.0315)


def dot_nt(a, b):
    return lax.dot_general(a, b, (((1,), (1,)), ((), ())), preferred_element_type=F32)


def dot_nn(a, b):
    return lax.dot_general(a, b, (((1,), (0,)), ((), ())), preferred_element_type=F32)


def dot_tn(a, b):
    return lax.dot_general(a, b, (((0,), (0,)), ((), ())), preferred_element_type=F32)


def split(x):
    high = x.astype(BF)
    return high, (x - high.astype(F32)).astype(BF)


def side(*parts):
    return jnp.concatenate(parts, axis=1)


def over(*parts):
    return jnp.concatenate(parts, axis=0)


def sigmoid(v):
    return 0.5 * (1.0 + jnp.tanh(0.5 * v))


def parts_of(x, fine):
    return split(x) if fine else (x.astype(BF),)


def left(parts):
    return side(parts[0], parts[1], parts[0]) if len(parts) == 2 else parts[0]


def right(parts, axis):
    if len(parts) == 1:
        return parts[0]
    return jnp.concatenate((parts[0], parts[0], parts[1]), axis=axis)


def newton_schulz(grads):
    xs = []
    for m in grads:
        norm = jnp.sqrt(jnp.sum(m * m, keepdims=True))
        xs.append(m * (1.0 / (norm + 1e-07)))
    for step in range(NS_ITERS):
        fine = step >= COARSE
        halves = [parts_of(x, fine) for x in xs]
        squares = [dot_nt(left(h), right(h, 1)) for h in halves]
        sq = [parts_of(a, fine) for a in squares]
        quartics = [dot_nn(left(a), right(a, 0)) for a in sq]
        mixing = [quintic_terms[1] * a + quintic_terms[2] * q for a, q in zip(squares, quartics)]
        xs = [
            quintic_terms[0] * x + dot_nn(left(parts_of(b, fine)), right(h, 0))
            for x, b, h in zip(xs, mixing, halves)
        ]
    return xs


def lengths(m, axis):
    return jnp.sqrt(jnp.sum(m * m, axis=axis, keepdims=True))


AXES = (1, 1, 0)


def kernel(
    dims,
    q_any, k_any, v_any, gate_any, up_any, down_any, gain_ref, step_ref, scale_ref,
    out_ref,
    q_ref, k_ref, v_ref, gate_ref, up_ref, down_ref, local_sem,
    kp, vp, here, before, mix, top, den, att, qn, comb, wb, wf, target, gp, rp, cs, rz, tot, fw, part, others,
    kv_send, kv_recv, pair_send, pair_recv, mate_send, mate_recv, fw_send, fw_recv,
    w_send, w_recv, head_send, head_recv,
):
    frames, nh, hd = dims
    rows, width = q_any.shape
    dh = width // hd
    half = frames // GROUPS
    mates = half // 2
    own = hd // 2
    p = lax.axis_index("frame")
    j = lax.axis_index("head")
    core = lax.rem(p, 2)
    seg = p // half
    rank = lax.rem(p, half) // 2
    pair = p + 1 - 2 * core
    has_prev = p > 0
    has_next = p < frames - 1
    prev_far = jnp.logical_and(core == 0, has_prev)
    next_far = jnp.logical_and(core == 1, has_next)

    locals_ = [
        pltpu.make_async_copy(src, dst, local_sem.at[n])
        for n, (src, dst) in enumerate(
            zip(
                (k_any, q_any, v_any, gate_any, up_any, down_any),
                (k_ref, q_ref, v_ref, gate_ref, up_ref, down_ref),
            )
        )
    ]

    def start_local():
        for copy in locals_:
            copy.start()

    def fw_targets(s):
        return [(to, r) for to in reversed(range(s + 1, GROUPS)) for r in reversed(range(mates))]

    barrier = pltpu.get_barrier_semaphore()

    def greet(frame_at, head_at):
        pl.semaphore_signal(barrier, inc=1, device_id=(frame_at, head_at), device_id_type=MESH)

    greet(pair, j)

    @pl.when(next_far)
    def _():
        greet(p + 1, j)

    @pl.when(prev_far)
    def _():
        greet(p - 1, j)

    def mate_at(step):
        return seg * half + 2 * lax.rem(rank + step, mates) + core

    def head_at(step):
        return lax.rem(j + step, nh)

    for step in range(1, mates):
        greet(mate_at(step), j)
    for step in range(1, nh):
        greet(p, head_at(step))
    is_last = rank == mates - 1
    for s in range(GROUPS):
        @pl.when(jnp.logical_and(is_last, seg == s))
        def _(s=s):
            for to, r in fw_targets(s):
                greet(to * half + 2 * r + core, j)

        @pl.when(seg > s)
        def _(s=s):
            greet(s * half + 2 * (mates - 1) + core, j)

    start_local()
    count = mates - 1 + nh - 1 + 1 + seg
    far = prev_far.astype(jnp.int32) + next_far.astype(jnp.int32)
    far = far + is_last.astype(jnp.int32) * (GROUPS - 1 - seg) * mates
    pl.semaphore_wait(barrier, count + far)

    ahead = jnp.minimum(p + 1, frames - 1)

    def kv_copy(h, which):
        src, dst = ((k_any, kp), (v_any, vp))[which]
        return pltpu.make_async_remote_copy(
            src_ref=src.at[:, pl.ds(h * dh, dh)],
            dst_ref=dst.at[h],
            send_sem=kv_send.at[2 * h + which],
            recv_sem=kv_recv.at[2 * h + which],
            device_id=(ahead, j),
            device_id_type=MESH,
        )

    @pl.when(has_next)
    def _():
        for which in range(2):
            for h in range(hd):
                kv_copy(h, which).start()

    factor = math.log2(math.e) / math.sqrt(dh)

    block = min(rows, 256)

    for copy in locals_:
        copy.wait()

    def exps(q, keys):
        scores = dot_nt(q, keys) * factor
        high = jnp.max(scores, axis=1, keepdims=True)
        e = jnp.exp2(scores - high)
        return e, high, jnp.sum(e, axis=1, keepdims=True)

    for h in range(hd):
        cols = slice(h * dh, (h + 1) * dh)
        for r in range(0, rows, block):
            rs = slice(r, r + block)
            e, t, d = exps(q_ref[rs, cols], k_ref[:, cols])
            here[h, rs] = e
            top[h, rs] = t
            den[h, rs] = d
        qf = q_ref[:, cols].astype(F32)
        mean = jnp.mean(qf * qf, axis=1, keepdims=True)
        qn[h] = (qf * lax.rsqrt(mean + 1e-06)).astype(BF)
        for m, ref in enumerate((gate_ref, up_ref, down_ref)):
            w = ref[h]
            w = w.T if AXES[m] else w
            high, low = split(w)
            wb[0, h, m] = side(high, low)
    for i in range(own):
        h = core * own + i
        for m, ref in enumerate((gate_ref, up_ref, down_ref)):
            w = ref[h]
            w = w.T if AXES[m] else w
            wf[i, m] = w
            target[i, m] = jnp.broadcast_to(lengths(w, AXES[m]), w.shape)

    @pl.when(has_prev)
    def _():
        for h in range(hd):
            cols = slice(h * dh, (h + 1) * dh)
            kv_copy(h, 0).wait_recv()
            for r in range(0, rows, block):
                rs = slice(r, r + block)
                e, t, d = exps(q_ref[rs, cols], kp[h])
                t0 = top[h, rs]
                high = jnp.maximum(t, t0)
                a, b = jnp.exp2(t0 - high), jnp.exp2(t - high)
                inv = 1.0 / (den[h, rs] * a + d * b)
                before[h, rs] = (e * (b * inv)).astype(BF)
                probs = (here[h, rs] * (a * inv)).astype(BF)
                mix[h, rs] = dot_nn(probs, v_ref[:, cols])

    @pl.when(jnp.logical_not(has_prev))
    def _():
        for h in range(hd):
            cols = slice(h * dh, (h + 1) * dh)
            for r in range(0, rows, block):
                rs = slice(r, r + block)
                probs = (here[h, rs] * (1.0 / den[h, rs])).astype(BF)
                mix[h, rs] = dot_nn(probs, v_ref[:, cols])

    for h in range(hd):
        @pl.when(has_prev)
        def _(h=h):
            kv_copy(h, 1).wait_recv()
            mix[h] = mix[h] + dot_nn(before[h], vp[h])

        m = mix[h]
        mean = jnp.mean(m * m, axis=1, keepdims=True)
        att[h] = (m * lax.rsqrt(mean + 1e-06)).astype(BF)

    def pair_copy(i, m):
        return pltpu.make_async_remote_copy(
            src_ref=gp.at[(1 - core) * own + i, m],
            dst_ref=rp.at[i, m],
            send_sem=pair_send.at[i * 3 + m],
            recv_sem=pair_recv.at[i * 3 + m],
            device_id=(pair, j),
            device_id_type=MESH,
        )

    def mate_copy(step, i, m):
        return pltpu.make_async_remote_copy(
            src_ref=cs.at[i, m],
            dst_ref=rz.at[step - 1, i, m],
            send_sem=mate_send.at[step - 1, i * 3 + m],
            recv_sem=mate_recv.at[step - 1, i * 3 + m],
            device_id=(mate_at(step), j),
            device_id_type=MESH,
        )

    def fw_copy(s, to, r, i, m):
        return pltpu.make_async_remote_copy(
            src_ref=cs.at[own + i, m],
            dst_ref=fw.at[s, i, m],
            send_sem=fw_send.at[(to - s - 1) * mates + r, i * 3 + m],
            recv_sem=fw_recv.at[s, i * 3 + m],
            device_id=(to * half + 2 * r + core, j),
            device_id_type=MESH,
        )

    def w_copy(state, i, m, which):
        at = which * own + i
        span = pl.ds(0, dh if state == GROUPS else 2 * dh)
        return pltpu.make_async_remote_copy(
            src_ref=wb.at[state, at, m, :, span],
            dst_ref=wb.at[state, at, m, :, span],
            send_sem=w_send.at[state - 1, i * 3 + m],
            recv_sem=w_recv.at[state - 1, i * 3 + m],
            device_id=(pair, j),
            device_id_type=MESH,
        )

    def fast_grads(state, h):
        x = att[h]
        y = v_ref[:, pl.ds(pl.multiple_of(h * dh, dh), dh)]
        xx = side(x, x)
        gate = dot_nt(wb[state, h, 0], xx)
        upward = dot_nt(wb[state, h, 1], xx)
        back = -dot_nt(wb[state, h, 2], side(y, y))
        sig = sigmoid(gate)
        active = gate * sig
        hidden = active * upward
        gp[h, 2] = -dot_nn(hidden.astype(BF), y)
        back_gate = back * upward * sig * (1.0 + gate * (1.0 - sig))
        gp[h, 0] = dot_nn(back_gate.astype(BF), x)
        gp[h, 1] = dot_nn((back * active).astype(BF), x)

    for s in range(GROUPS):
        @pl.when(seg == s)
        def _(s=s):
            for i in range(own):
                fast_grads(s, (1 - core) * own + i)
                for m in range(3):
                    pair_copy(i, m).start()
            for i in range(own):
                fast_grads(s, core * own + i)
            for i in range(own):
                for m in range(3):
                    pair_copy(i, m).wait_recv()
                    chip = gp[core * own + i, m] + rp[i, m]
                    cs[i, m] = chip.astype(SENT)
                    for step in range(1, mates):
                        mate_copy(step, i, m).start()
                    tot[i, m] = chip
            for i in range(own):
                for m in range(3):
                    total = tot[i, m]
                    for step in range(1, mates):
                        mate_copy(step, i, m).wait_recv()
                        total = total + rz[step - 1, i, m].astype(F32)
                    tot[i, m] = total
                    if s < GROUPS - 1:
                        cs[own + i, m] = total.astype(SENT)

                        @pl.when(rank == mates - 1)
                        def _(i=i, m=m):
                            fw_copy(s, *fw_targets(s)[0], i, m).start()

            if s < GROUPS - 1:
                @pl.when(rank == mates - 1)
                def _():
                    for to, r in fw_targets(s)[1:]:
                        for i in range(own):
                            for m in range(3):
                                fw_copy(s, to, r, i, m).start()

        if s < GROUPS - 1:
            @pl.when(seg > s)
            def _(s=s):
                for i in range(own):
                    for m in range(3):
                        fw_copy(s, s + 1, 0, i, m).wait_recv()
                        tot[i, m] = fw[s, i, m].astype(F32)

        @pl.when(seg >= s)
        def _(s=s):
            for i in range(own):
                at = core * own + i
                rate = step_ref[at]
                ortho = newton_schulz([tot[i, m] for m in range(3)])
                for m in range(3):
                    moved = wf[i, m] - rate * ortho[m]
                    w = moved * (target[i, m] / (lengths(moved, AXES[m]) + 1e-06))
                    if s < GROUPS - 1:
                        wf[i, m] = w
                    high, low = split(w)
                    wb[s + 1, at, m] = side(high, low)
                    w_copy(s + 1, i, m, core).start()
            for i in range(own):
                for m in range(3):
                    w_copy(s + 1, i, m, 1 - core).wait_recv()

    ones = jnp.ones((8, dh), BF)
    sums = jnp.zeros((8, rows), F32)
    mine = seg + 1
    for h in range(hd):
        cols = slice(h * dh, (h + 1) * dh)
        x = qn[h]
        gate = dot_nt(x, wb[mine, h, 0][:, :dh])
        upward = dot_nt(x, wb[mine, h, 1][:, :dh])
        hidden = (gate * sigmoid(gate) * upward).astype(BF)
        out = dot_nn(hidden, wb[mine, h, 2][:, :dh])
        fast = (out * scale_ref[h]).astype(BF)
        both = att[h].astype(F32) + fast.astype(F32)
        comb[:, cols] = both
        high, low = split(both * both)
        sums = sums + dot_nt(side(ones, ones), side(high, low))
    sums = jnp.maximum(sums, 0.0)
    part[...] = sums

    def head_copy(step):
        return pltpu.make_async_remote_copy(
            src_ref=part,
            dst_ref=others.at[step - 1],
            send_sem=head_send.at[step - 1],
            recv_sem=head_recv.at[step - 1],
            device_id=(p, head_at(step)),
            device_id_type=MESH,
        )

    for step in range(1, nh):
        head_copy(step).start()
    for step in range(1, nh):
        head_copy(step).wait_recv()
        sums = sums + others[step - 1]
    high, low = split(lax.rsqrt(sums / (width * nh) + 1e-05))
    eighths = jnp.full((16, dh), 0.125, BF)
    inverse = dot_tn(over(high.astype(F32), low.astype(F32)).astype(BF), eighths)
    for h in range(hd):
        cols = slice(h * dh, (h + 1) * dh)
        out_ref[:, cols] = comb[:, cols] * inverse

    for step in range(1, nh):
        head_copy(step).wait_send()

    @pl.when(has_next)
    def _():
        for h in range(hd):
            for which in range(2):
                kv_copy(h, which).wait_send()

    for i in range(own):
        for m in range(3):
            pair_copy(i, m).wait_send()
            for step in range(1, mates):
                mate_copy(step, i, m).wait_send()
    for s in range(GROUPS):
        @pl.when(seg >= s)
        def _(s=s):
            for i in range(own):
                for m in range(3):
                    w_copy(s + 1, i, m, core).wait_send()

        if s < GROUPS - 1:
            @pl.when(jnp.logical_and(seg == s, rank == mates - 1))
            def _(s=s):
                for to, r in fw_targets(s):
                    for i in range(own):
                        for m in range(3):
                            fw_copy(s, to, r, i, m).wait_send()


def shards(
    queries, key_rows, values, gate_init, up_init, down_init, step_size, head_scale, out_gain
):
    rows, width = queries.shape
    hd, dh, fwh = gate_init.shape
    frames, nh = lax.axis_size("frame"), lax.axis_size("head")
    mates = frames // GROUPS // 2
    own = hd // 2
    dma = pltpu.SemaphoreType.DMA
    vmem = pl.BlockSpec(memory_space=pltpu.VMEM)
    smem = pl.BlockSpec(memory_space=pltpu.SMEM)
    scaled = pl.pallas_call(
        functools.partial(kernel, (frames, nh, hd)),
        out_shape=jax.ShapeDtypeStruct((rows, width), F32),
        in_specs=[pl.BlockSpec(memory_space=pl.ANY)] * 6 + [vmem] + [smem] * 2,
        out_specs=vmem,
        scratch_shapes=[
            pltpu.VMEM((rows, width), BF),
            pltpu.VMEM((rows, width), BF),
            pltpu.VMEM((rows, width), BF),
            pltpu.VMEM((hd, dh, fwh), F32),
            pltpu.VMEM((hd, dh, fwh), F32),
            pltpu.VMEM((hd, fwh, dh), F32),
            dma((6,)),
            pltpu.VMEM((hd, rows, dh), BF),
            pltpu.VMEM((hd, rows, dh), BF),
            pltpu.VMEM((hd, rows, rows), F32),
            pltpu.VMEM((hd, rows, rows), BF),
            pltpu.VMEM((hd, rows, dh), F32),
            pltpu.VMEM((hd, rows, 1), F32),
            pltpu.VMEM((hd, rows, 1), F32),
            pltpu.VMEM((hd, rows, dh), BF),
            pltpu.VMEM((hd, rows, dh), BF),
            pltpu.VMEM((rows, width), F32),
            pltpu.VMEM((GROUPS + 1, hd, 3, dh, 2 * fwh), BF),
            pltpu.VMEM((own, 3, dh, fwh), F32),
            pltpu.VMEM((own, 3, dh, fwh), F32),
            pltpu.VMEM((hd, 3, dh, fwh), F32),
            pltpu.VMEM((own, 3, dh, fwh), F32),
            pltpu.VMEM((2 * own, 3, dh, fwh), SENT),
            pltpu.VMEM((max(mates - 1, 1), own, 3, dh, fwh), SENT),
            pltpu.VMEM((own, 3, dh, fwh), F32),
            pltpu.VMEM((GROUPS - 1, own, 3, dh, fwh), SENT),
            pltpu.VMEM((8, rows), F32),
            pltpu.VMEM((max(nh - 1, 1), 8, rows), F32),
            dma((2 * hd,)), dma((2 * hd,)),
            dma((own * 3,)), dma((own * 3,)),
            dma((max(mates - 1, 1), own * 3)), dma((max(mates - 1, 1), own * 3)),
            dma(((GROUPS - 1) * mates, own * 3)), dma((GROUPS - 1, own * 3)),
            dma((GROUPS, own * 3)), dma((GROUPS, own * 3)),
            dma((max(nh - 1, 1),)), dma((max(nh - 1, 1),)),
        ],
        compiler_params=pltpu.CompilerParams(
            collective_id=0, has_side_effects=True, vmem_limit_bytes=56 * 1024 * 1024
        ),
    )(
        queries, key_rows, values, gate_init, up_init, down_init,
        out_gain.reshape(1, width), step_size, head_scale,
    )
    return (scaled * out_gain[None, :]).astype(BF)


def solution(mesh):
    in_specs = (
        P("frame", "head"),
        P("frame", "head"),
        P("frame", "head"),
        P("head", None, None),
        P("head", None, None),
        P("head", None, None),
        P("head"),
        P("head"),
        P("head"),
    )
    return jax.shard_map(
        shards, mesh=mesh, in_specs=in_specs, out_specs=P("frame", "head"), check_vma=False
    )
```
